32 devices in a mesh: leaf: 4 (over y, x), row: 2 (over core), col: 4 (over z).
Axes of the slice: x: 2, y: 2, z: 4, core: 2. Of those that a mesh axis runs over, the one named last changes fastest.
Arguments:
- root_inverse: float32 [4096, 4096], P('row', ('leaf', 'col')), may hold values from -48 to 48, as said below
- lower_panel: float32 [4, 4096, 4096], P('leaf', 'row', 'col'), may hold values from -0.375 to 0.375
- panel_mask: int32 [4, 16, 16], P('leaf', 'row', 'col'), may hold values from 0 to 1, as said below
- factor_inverse: float32 [4, 4096, 4096], P('leaf', 'row', 'col'), may hold values from -8 to 8, as said below
Outputs:
- cross_inverse: float32 [4, 4096, 4096], P('leaf', 'row', 'col')
- block_inverse: float32 [4, 4096, 4096], P('leaf', 'row', 'col')
The draws below stay inside these ranges and needn't reach their ends.
Inputs may be any that keep to these rules, and one draw needn't show every extreme that they name: `panel_mask`: each entry says whether the 256 x 256 block of a child's panel is kept; the share of kept blocks differs from block row to block row. `root_inverse`: symmetric and positive definite. `factor_inverse`: each child's matrix is symmetric and positive definite.
All inputs are finite; a program needn't handle non-finite values.
Results may differ from the reference program's by a relative error of at most 0.0001.
Values sent between devices are 32-bit elements; how exact they have to be, the bound alone decides.
A program may use at most 256 MiB of HBM per device.

```python
import math
import jax
import jax.numpy as jnp
from jax import lax

BS = 256
NR = 4096
NC = 4096
CHILDREN = 4
RB = 16
CB = 16


def draw_root_inverse(key, part):
    keys = jax.random.split(key, 2)
    raw = jax.random.truncated_normal(keys[0], -6.0, 6.0, (NR, NR), jnp.float32)
    coupling = (raw + raw.T) * (0.35 / math.sqrt(NR))
    identity = (lax.broadcasted_iota(jnp.int32, (NR, NR), 0) == lax.broadcasted_iota(jnp.int32, (NR, NR), 1)).astype(jnp.float32)
    diagonal = jax.random.uniform(keys[1], (NR,), jnp.float32, 1.5, 3.0)
    matrix = coupling * (1.0 - identity) + identity * diagonal[None, :]
    return matrix


def draw_factor_inverse(key, part):
    keys = jax.random.split(key, 2)
    raw = jax.random.truncated_normal(keys[0], -6.0, 6.0, (CHILDREN, NC, NC), jnp.float32)
    coupling = (raw + jnp.swapaxes(raw, 1, 2)) * (0.2 / math.sqrt(NC))
    identity = (lax.broadcasted_iota(jnp.int32, (1, NC, NC), 1) == lax.broadcasted_iota(jnp.int32, (1, NC, NC), 2)).astype(jnp.float32)
    diagonal = jax.random.uniform(keys[1], (CHILDREN, 1, NC), jnp.float32, 1.0, 2.0)
    matrix = coupling * (1.0 - identity) + identity * diagonal
    return matrix


def draw_panel_mask(key, part):
    keys = jax.random.split(key, 2)
    level = jax.random.randint(keys[0], (CHILDREN, RB, 1), 0, 9)
    coins = jax.random.randint(keys[1], (CHILDREN, RB, CB), 0, 8)
    return (coins < level).astype(jnp.int32)


def level_of(key, shape, shards, least, high):
    level, own = 1.0, jax.random.fold_in(key, 6)
    for position, shards_of in shards:
        steps = jnp.exp(jax.random.uniform(jax.random.fold_in(own, position), (shards_of,), jnp.float32, least / len(shards), high / len(shards)))
        level = level * jnp.repeat(steps, shape[position] // shards_of).reshape([-1 if axis == position else 1 for axis in range(len(shape))])
    return level


def bell_draw(own_key, dims, width, most, cuts=(), kind=jnp.bfloat16):
    entries = width * jax.random.normal(own_key, dims, jnp.float32)
    if cuts:
        entries = entries * level_of(own_key, dims, cuts, -0.22, 0.18)
    return jnp.clip(entries, -most, most).astype(kind)


def setup_inputs(seed: int = 0) -> dict:
    arg_keys = jax.random.split(jax.random.key(seed), 5)
    return {
        "root_inverse": draw_root_inverse(jax.random.fold_in(arg_keys[4], 71), 0),
        "lower_panel": bell_draw(arg_keys[1], (CHILDREN, NR, NC), (NR // 16) ** -0.5, 0.375, ((0, 4), (1, 2), (2, 4)), jnp.float32),
        "panel_mask": draw_panel_mask(jax.random.fold_in(arg_keys[4], 71), 0),
        "factor_inverse": draw_factor_inverse(jax.random.fold_in(arg_keys[4], 71), 0),
    }


def spread(mask):
    return jnp.repeat(jnp.repeat(mask.astype(jnp.float32), BS, axis=1), BS, axis=2)


def reference(root_inverse, lower_panel, panel_mask, factor_inverse):
    pattern = spread(panel_mask)
    masked = lower_panel * pattern
    crosses = []
    blocks = []
    for kid_index in range(CHILDREN):
        ancestor = jnp.dot(root_inverse, masked[kid_index], precision=lax.Precision.HIGHEST, preferred_element_type=jnp.float32)
        crosses.append(-(ancestor * pattern[kid_index]))
        blocks.append(factor_inverse[kid_index] + jnp.dot(masked[kid_index].T, ancestor, precision=lax.Precision.HIGHEST, preferred_element_type=jnp.float32))
    return jnp.stack(crosses), jnp.stack(blocks)
```

```python
import math

import jax
import jax.numpy as jnp
from jax import lax
from jax.sharding import PartitionSpec as P


BS = 256
CHUNKS = 2


def mul_t(left, right):
    return lax.dot_general(
        left,
        right,
        (((0,), (0,)), ((), ())),
        precision=lax.Precision.HIGH,
        preferred_element_type=jnp.float32,
    )


def pattern_of(mask):
    return jnp.repeat(mask.astype(jnp.float32), BS, axis=1)[:, None, :]


def masked_by(values, pattern):
    rows, cols = values.shape
    return (values.reshape(-1, BS, cols) * pattern).reshape(rows, cols)


def make_per_device(n_row, n_col):
    def per_device(root_inverse, lower_panel, panel_mask, factor_inverse):
        me = lax.axis_index("col")
        row = lax.axis_index("row")
        pattern = pattern_of(panel_mask[0])
        own = masked_by(lower_panel[0], pattern)
        width = own.shape[1]
        ring = [(i, (i + 1) % n_col) for i in range(n_col)]

        root_cols = lax.all_gather(root_inverse, "col", axis=1, tiled=True)
        first, root_cols = lax.optimization_barrier((own, root_cols))
        panels = [first]
        for _ in range(1, n_col // 2):
            panels.append(lax.ppermute(panels[-1], "col", ring))

        column_panel = lax.all_gather(own, "row", axis=0, tiled=True)
        n_rows = root_inverse.shape[0]
        chunks = math.gcd(CHUNKS, n_rows // 8)
        step = n_rows // chunks
        pieces = []
        for c in range(chunks):
            root_rows = lax.all_gather(
                root_cols[c * step : (c + 1) * step], "leaf", axis=1, tiled=True
            )
            if c == 0:
                root_rows, *panels = lax.optimization_barrier((root_rows, *panels))
                if n_col > 1:
                    panels.append(lax.ppermute(panels[-1], "col", ring))
            pieces.append(
                jnp.dot(
                    root_rows,
                    column_panel,
                    precision=lax.Precision.HIGH,
                    preferred_element_type=jnp.float32,
                )
            )
        ancestor = jnp.concatenate(pieces, axis=0)
        cross_inverse = -masked_by(ancestor, pattern)[None]

        partial = jnp.zeros((n_col * width, width), jnp.float32)
        share = width // n_row

        def put(total, block, place, offset=0):
            return lax.dynamic_update_slice_in_dim(total, block, place * width + offset, 0)

        returned = []
        nearer = [d for d in range(1, n_col // 2 + 1) if 2 * d < n_col]
        for d in nearer:
            block = mul_t(ancestor, panels[d])
            summed = lax.psum_scatter(block, "row", scatter_dimension=0, tiled=True)
            back = [(i, (i - d) % n_col) for i in range(n_col)]
            returned.append((d, lax.ppermute(summed, "col", back)))
            partial = put(partial, block.T, lax.rem(me - d + n_col, n_col))
        for d in range(n_col // 2 + 1):
            if d not in nearer:
                block = mul_t(panels[d], ancestor)
                partial = put(partial, block, lax.rem(me - d + n_col, n_col))
        for d, block in returned:
            partial = put(partial, block, lax.rem(me + d, n_col), row * share)

        reduced = lax.psum_scatter(partial, "row", scatter_dimension=0, tiled=True)
        return cross_inverse, factor_inverse + reduced[None]

    return per_device


def solution(mesh):
    in_specs = (
        P("row", ("leaf", "col")),
        P("leaf", "row", "col"),
        P("leaf", "row", "col"),
        P("leaf", "row", "col"),
    )
    out_specs = (P("leaf", "row", "col"), P("leaf", "row", "col"))
    return jax.shard_map(
        make_per_device(mesh.shape["row"], mesh.shape["col"]),
        mesh=mesh,
        in_specs=in_specs,
        out_specs=out_specs,
        check_vma=False,
    )
```

```python
import math

import jax
import jax.numpy as jnp
from jax import lax
from jax.sharding import PartitionSpec as P


BS = 256
CHUNKS = 2


def mul_t(left, right):
    return lax.dot_general(
        left,
        right,
        (((0,), (0,)), ((), ())),
        precision=lax.Precision.HIGH,
        preferred_element_type=jnp.float32,
    )


def pattern_of(mask):
    return jnp.repeat(mask.astype(jnp.float32), BS, axis=1)[:, None, :]


def masked_by(values, pattern):
    rows, cols = values.shape
    return (values.reshape(-1, BS, cols) * pattern).reshape(rows, cols)


def make_per_device(n_row, n_col):
    def per_device(root_inverse, lower_panel, panel_mask, factor_inverse):
        me = lax.axis_index("col")
        row = lax.axis_index("row")
        pattern = pattern_of(panel_mask[0])
        own = masked_by(lower_panel[0], pattern)
        width = own.shape[1]
        ring = [(i, (i + 1) % n_col) for i in range(n_col)]

        root_cols = lax.all_gather(root_inverse, "col", axis=1, tiled=True)
        first, root_cols = lax.optimization_barrier((own, root_cols))
        panels = [first]
        for _ in range(1, n_col // 2):
            panels.append(lax.ppermute(panels[-1], "col", ring))

        column_panel = lax.all_gather(own, "row", axis=0, tiled=True)
        n_rows = root_inverse.shape[0]
        chunks = math.gcd(CHUNKS, n_rows // 8)
        step = n_rows // chunks
        pieces = []
        nearer = [d for d in range(1, n_col // 2 + 1) if 2 * d < n_col]
        blocks = {}
        for c in range(chunks):
            root_rows = lax.all_gather(
                root_cols[c * step : (c + 1) * step], "leaf", axis=1, tiled=True
            )
            if c == 0:
                root_rows, *panels = lax.optimization_barrier((root_rows, *panels))
                if n_col > 1:
                    panels.append(lax.ppermute(panels[-1], "col", ring))
            pieces.append(
                jnp.dot(
                    root_rows,
                    column_panel,
                    precision=lax.Precision.HIGH,
                    preferred_element_type=jnp.float32,
                )
            )
            for d in range(max(n_col // 2, 1)):
                rows = panels[d][c * step : (c + 1) * step]
                pair = (pieces[-1], rows) if d in nearer else (rows, pieces[-1])
                term = mul_t(*pair)
                blocks[d] = blocks[d] + term if c else lax.optimization_barrier(term)
        ancestor = jnp.concatenate(pieces, axis=0)
        cross_inverse = -masked_by(ancestor, pattern)[None]

        partial = jnp.zeros((n_col * width, width), jnp.float32)
        share = width // n_row

        def put(total, block, place, offset=0):
            return lax.dynamic_update_slice_in_dim(total, block, place * width + offset, 0)

        returned = []
        for d in nearer:
            if d not in blocks:
                blocks[d] = mul_t(ancestor, panels[d])
            summed = lax.psum_scatter(blocks[d], "row", scatter_dimension=0, tiled=True)
            back = [(i, (i - d) % n_col) for i in range(n_col)]
            returned.append((d, lax.ppermute(summed, "col", back)))
            partial = put(partial, blocks[d].T, lax.rem(me - d + n_col, n_col))
        for d in range(n_col // 2 + 1):
            if d not in nearer:
                block = blocks[d] if d in blocks else mul_t(panels[d], ancestor)
                partial = put(partial, block, lax.rem(me - d + n_col, n_col))
        for d, block in returned:
            partial = put(partial, block, lax.rem(me + d, n_col), row * share)

        reduced = lax.psum_scatter(partial, "row", scatter_dimension=0, tiled=True)
        return cross_inverse, factor_inverse + reduced[None]

    return per_device


def solution(mesh):
    in_specs = (
        P("row", ("leaf", "col")),
        P("leaf", "row", "col"),
        P("leaf", "row", "col"),
        P("leaf", "row", "col"),
    )
    out_specs = (P("leaf", "row", "col"), P("leaf", "row", "col"))
    return jax.shard_map(
        make_per_device(mesh.shape["row"], mesh.shape["col"]),
        mesh=mesh,
        in_specs=in_specs,
        out_specs=out_specs,
        check_vma=False,
    )
```
